512 devices in a mesh: tm: 64 (over x, y, core), row: 8 (over z).
Axes of the slice: x: 4, y: 8, z: 8, core: 2. Of those that a mesh axis runs over, the one named last changes fastest.
Arguments:
- trans: bfloat16 [128, 1024, 1024], P('tm', 'row'), may hold values from -0.3 to 0.9
- offset: bfloat16 [128, 1024], P('tm', 'row'), may hold values from -6 to 6
- spread: bfloat16 [128, 1024, 1024], P('tm', 'row'), may hold values from -0.3 to 2.3, as said below
Outputs:
- trans_out: bfloat16 [128, 1024, 1024], P('tm', 'row')
- offset_out: bfloat16 [128, 1024], P('tm', 'row')
- spread_out: bfloat16 [128, 1024, 1024], P('tm', 'row')
The draws below stay inside these ranges and needn't reach their ends.
Inputs may be any that keep to these rules, and one draw needn't show every extreme that they name: `spread`: each block's matrix is symmetric.
All inputs are finite; a program needn't handle non-finite values.
Results may differ from the reference program's by a relative error of at most 0.0056.
Values may be sent and summed in bfloat16 or wider, within the bound.
No kernel may reach another device: no remote copies, remote signals or barrier semaphores. Data moves between devices by JAX's collectives and lax.ppermute only.
A program may use at most 64 MiB of HBM per device.

```python
import math
import jax
import jax.numpy as jnp
from jax import lax

D = 1024
LEVELS = 2
BLOCKS = 128


def draw_trans(key, part):
    jitter = jax.random.normal(key, (BLOCKS, D, D), jnp.float32)
    jitter = jnp.clip(jitter, -4.0, 4.0) * (0.5 / math.sqrt(D))
    identity = jnp.eye(D, dtype=jnp.float32)
    return (0.6 * identity[None] + jitter).astype(jnp.bfloat16)


def draw_spread(key, part):
    matrix = jax.random.normal(jax.random.fold_in(key, 1), (BLOCKS, D, D), jnp.float32)
    matrix = jnp.clip(matrix, -4.0, 4.0) * (0.5 / math.sqrt(D))
    symmetric = 0.5 * (matrix + jnp.swapaxes(matrix, 1, 2))
    diagonal = jnp.exp(jax.random.uniform(jax.random.fold_in(key, 2), (BLOCKS, D), jnp.float32, math.log(0.5), math.log(2.0)))
    identity = jnp.eye(D, dtype=jnp.float32)
    return (symmetric + diagonal[:, :, None] * identity[None]).astype(jnp.bfloat16)


def levels(own_key, extent, split, least, high):
    factor_of, own = 1.0, jax.random.fold_in(own_key, 6)
    for position, blocks in split:
        heights = jnp.exp(jax.random.uniform(jax.random.fold_in(own, position), (blocks,), jnp.float32, least / len(split), high / len(split)))
        factor_of = factor_of * jnp.repeat(heights, extent[position] // blocks).reshape([-1 if axis == position else 1 for axis in range(len(extent))])
    return factor_of


def normal_values(rng, shape, scale, most, pieces=(), kind=jnp.bfloat16):
    entries = jax.random.normal(rng, shape, jnp.float32) * scale
    if len(pieces) > 0:
        entries = levels(rng, shape, pieces, -0.22, 0.18) * entries
    return jnp.clip(entries, min=-most, max=most).astype(kind)


def setup_inputs(seed: int = 0) -> dict:
    arg_keys = jax.random.split(jax.random.key(seed), 4)
    return {
        "trans": draw_trans(jax.random.fold_in(arg_keys[3], 71), 0),
        "offset": normal_values(arg_keys[1], (BLOCKS, D), 1.0, 6.0, ((0, 64), (1, 8))),
        "spread": draw_spread(jax.random.fold_in(arg_keys[3], 71), 0),
    }


def compose(left_trans, left_offset, left_spread, right_trans, right_offset, right_spread):
    trans_left = left_trans.astype(jnp.float32)
    trans_right = right_trans.astype(jnp.float32)
    new_trans = jnp.einsum("bik,bkj->bij", trans_left, trans_right).astype(jnp.bfloat16)
    new_offset = (jnp.einsum("bik,bk->bi", trans_left, right_offset.astype(jnp.float32)) + left_offset.astype(jnp.float32)).astype(jnp.bfloat16)
    partial_value = jnp.einsum("bik,bkj->bij", trans_left, right_spread.astype(jnp.float32))
    partial_value = lax.optimization_barrier(partial_value.astype(jnp.bfloat16)).astype(jnp.float32)
    new_spread = (jnp.einsum("bik,bjk->bij", partial_value, trans_left) + left_spread.astype(jnp.float32)).astype(jnp.bfloat16)
    return new_trans, new_offset, new_spread


def reference(trans, offset, spread):
    for doubling in range(LEVELS):
        stride = 2 ** doubling
        leading = BLOCKS - stride
        merged = compose(trans[:leading], offset[:leading], spread[:leading], trans[stride:], offset[stride:], spread[stride:])
        trans = jnp.concatenate([merged[0], trans[leading:]], axis=0)
        offset = jnp.concatenate([merged[1], offset[leading:]], axis=0)
        spread = jnp.concatenate([merged[2], spread[leading:]], axis=0)
    return trans, offset, spread
```

```python
import jax
import jax.numpy as jnp
from jax import lax
from jax.experimental import pallas as pl
from jax.experimental.pallas import tpu as pltpu
from jax.sharding import PartitionSpec as P


BF16, F32 = jnp.bfloat16, jnp.float32
HBM = pl.BlockSpec(memory_space=pl.ANY)
VMEM = pl.BlockSpec(memory_space=pltpu.VMEM)
TAIL = 16


def hop(block, axis, distance):
    size = lax.axis_size(axis)
    return lax.ppermute(block, axis, [(i, (i + distance) % size) for i in range(size)])


def ring(block, turns, longer):
    pieces = [(0, block)]
    ahead = {1: block, -1: block}
    for turn in range(turns):
        for way in (1, -1):
            if turn < turns - 1 or way == longer:
                ahead[way] = hop(ahead[way], "row", way)
                pieces.append((-way * (turn + 1), ahead[way]))
    return pieces


def nn(a, b):
    return lax.dot_general(a, b, (((1,), (0,)), ((), ())), preferred_element_type=F32)


def nt(a, b):
    return lax.dot_general(a, b, (((1,), (1,)), ((), ())), preferred_element_type=F32)


def call(body, ins, outs, scratch, flops):
    return pl.pallas_call(
        body,
        in_specs=[spec for _, spec in ins],
        out_specs=tuple(VMEM for _ in outs),
        out_shape=tuple(jax.ShapeDtypeStruct(shape, kind) for shape, kind in outs),
        scratch_shapes=scratch,
        cost_estimate=pl.CostEstimate(flops=flops, bytes_accessed=8 * 2**20, transcendentals=0),
    )(*[array for array, _ in ins])


class Whole:
    def __init__(self, pieces, space, sems, count, by_panel=False):
        z = lax.axis_index("row")
        self.space, self.copies = space, []
        rows = space.shape[0] // count
        for n, (offset, ref) in enumerate(pieces):
            source = lax.rem(z + (offset + count), count)
            if by_panel:
                target = space.at[source]
            else:
                target = space.at[pl.ds(pl.multiple_of(source * rows, rows), rows), :]
            self.copies.append(pltpu.make_async_copy(ref, target, sems.at[n]))
        for copy in self.copies:
            copy.start()

    def wait(self):
        for copy in self.copies:
            copy.wait()
        return self.space


def unpack(packed, whole, count):
    size = whole.shape[0] // count
    half = count // 2
    for s in range(count):
        for k in range(half):
            c = (s + k) % count
            whole[s * size : (s + 1) * size, c * size : (c + 1) * size] = packed[s, k * size : (k + 1) * size, :]
        a, part = s % half, (size // 2) * (s // half)
        whole[a * size + part : a * size + part + size // 2, (a + half) * size : (a + half + 1) * size] = packed[
            s, half * size : half * size + size // 2, :
        ]
        for k in range(half + 1, count):
            c = (s + k) % count
            whole[s * size : (s + 1) * size, c * size : (c + 1) * size] = jnp.zeros((size, size), BF16)
        if s >= half:
            c = s - half
            whole[s * size : (s + 1) * size, c * size : (c + 1) * size] = jnp.zeros((size, size), BF16)


def by_symmetric(a, whole):
    return nn(a, whole) + nt(a, whole)


def two_rows(row):
    high = row.astype(BF16).astype(F32)
    index = lax.broadcasted_iota(jnp.int32, (TAIL, row.shape[1]), 0)
    return jnp.where(index == 0, high, jnp.where(index == 1, row - high, 0.0)).astype(BF16)


def one_row(tile):
    return tile[0:1].astype(F32) + tile[1:2].astype(F32)


def on_device(trans, offset, spread):
    count = lax.axis_size("row")
    _, rows, size = trans.shape
    half = count // 2
    packed_rows = half * rows + rows // 2
    one_product = 2 * rows * size * size
    panel, pair = ((rows, size), BF16), ((2 * rows, size), BF16)
    message = ((2 * rows + TAIL, size), BF16)

    fore, back = [trans], [trans]
    for _ in range(half - 1):
        fore.append(hop(fore[-1], "row", 1))
        back.append(hop(back[-1], "row", -1))
    last_even = hop(fore[-1][0], "row", 1)
    last_odd = hop(back[-1][1], "row", -1)
    turned = [(-k, fore[k]) for k in range(1, half)] + [(k, back[k]) for k in range(1, half)]
    e_arrays = [trans] + [array for _, array in turned] + [last_even, last_odd]
    e_offsets = [0] + [way for way, _ in turned]
    n_e = len(e_arrays)

    def e_pieces(refs, b):
        pieces = [(way, ref.at[b]) for way, ref in zip(e_offsets, refs)]
        return pieces + [(half, refs[n_e - 2 + b])]

    e_ins = [(array, HBM) for array in e_arrays]
    e_space = [pltpu.VMEM((size, size), BF16), pltpu.SemaphoreType.DMA((count,))]
    l_space = [
        pltpu.VMEM((size, size), BF16),
        pltpu.SemaphoreType.DMA((count,)),
    ]

    def pack(l_ref, g_ref, _, even_ref, odd_ref):
        z = lax.axis_index("row")
        for b, out in ((0, even_ref), (1, odd_ref)):
            for k in range(half):
                c = lax.rem(z + k, count)
                tile = l_ref[b, :, pl.ds(pl.multiple_of(c * rows, rows), rows)]
                out[k * rows : (k + 1) * rows, :] = tile * jnp.asarray(0.5, BF16) if k == 0 else tile
            c = lax.rem(z + half, count)
            tile = l_ref[b, :, pl.ds(pl.multiple_of(c * rows, rows), rows)].astype(F32)
            lower = tile.T[rows // 2 :]
            out[half * rows : packed_rows, :] = jnp.where(z < half, tile[: rows // 2], lower).astype(BF16)
        g = g_ref[...].astype(F32)
        index = lax.broadcasted_iota(jnp.int32, (TAIL, rows), 0)
        tile = jnp.where(index == 0, g[0:1], jnp.where(index == 1, g[1:2], 0.0))
        even_ref[packed_rows:, :] = tile.astype(BF16)

    even, odd = call(
        pack,
        [(spread, VMEM), (offset, VMEM), (fore[1], HBM)],
        [((packed_rows + TAIL, rows), BF16), ((packed_rows, rows), BF16)],
        [],
        1000,
    )
    even_ring, odd_ring = ring(even, half, 1), ring(odd, half, -1)
    even_ins = [(array, HBM) for _, array in even_ring]
    odd_ins = [(array, HBM) for _, array in odd_ring]
    even_packed = pltpu.VMEM((count, packed_rows + TAIL, rows), BF16)
    odd_packed = pltpu.VMEM((count, packed_rows, rows), BF16)

    def named(ring_, refs):
        return [(way, ref) for (way, _), ref in zip(ring_, refs)]

    def offsets_of(packed):
        return jnp.concatenate([packed[s, packed_rows:, :] for s in range(count)], axis=1)

    def first(*refs):
        own, out, space, sems = refs[n_e], refs[n_e + 1], refs[n_e + 2], refs[n_e + 3]
        e_odd = Whole(e_pieces(refs[:n_e], 1), space, sems, count).wait()
        out[...] = nn(own[0], e_odd[...]).astype(BF16)

    (x1,) = call(first, e_ins + [(trans, VMEM)], [panel], e_space, one_product)
    b1_in = hop(trans[1], "tm", 1)
    x1_in = hop(x1, "tm", 1)

    def second(*refs):
        x1_ref, b1_ref, x3_ref, b3_ref, x2_ref, even_e, even_s, odd_e, odd_s = refs[n_e:]
        e_even = Whole(e_pieces(refs[:n_e], 0), even_e, even_s, count)
        e_odd = Whole(e_pieces(refs[:n_e], 1), odd_e, odd_s, count)
        past = lax.axis_index("tm") < 1
        one = jnp.concatenate([x1_ref[...], b1_ref[...]], axis=0)
        two = nn(one, e_even.wait()[...]).astype(BF16)
        three = nn(two, e_odd.wait()[...])
        three = jnp.where(past, one.astype(F32), three).astype(BF16)
        x3_ref[...] = three[:rows]
        b3_ref[...] = three[rows:]
        x2_ref[...] = two

    x3, b3, x2 = call(
        second, e_ins + [(x1_in, VMEM), (b1_in, VMEM)], [panel, panel, pair], e_space + e_space, 4 * one_product
    )
    b3_in = hop(b3, "tm", 1)

    def third(*refs):
        l_refs = refs[n_e : n_e + count]
        b3_ref, x3_ref, b4_ref, m_ref, space, sems, packed, l_even, l_sems = refs[n_e + count :]
        l_copy = Whole(named(even_ring, l_refs), packed, l_sems, count, True)
        e_even = Whole(e_pieces(refs[:n_e], 0), space, sems, count)
        past = lax.axis_index("tm") < 2
        own = b3_ref[...]
        l_copy.wait()
        unpack(packed, l_even, count)
        v = jnp.where(past, 0.0, by_symmetric(own, l_even[...]))
        v_row = jnp.where(past, 0.0, nt(offsets_of(packed), own)[0:1])
        m_ref[:rows, :] = x3_ref[...]
        m_ref[rows : 2 * rows, :] = v.astype(BF16)
        m_ref[2 * rows :, :] = jnp.zeros((TAIL, size), BF16)
        m_ref[2 * rows :, :rows] = two_rows(v_row)
        b4 = nn(own, e_even.wait()[...])
        b4_ref[...] = jnp.where(past, own.astype(F32), b4).astype(BF16)

    b4, m1 = call(
        third,
        e_ins + even_ins + [(b3_in, VMEM), (x3, VMEM)],
        [panel, message],
        e_space + [even_packed] + l_space,
        3 * one_product,
    )
    b4_in = hop(b4, "tm", -2)
    m1_in = hop(m1, "tm", -1)

    def fourth(*refs):
        l_refs = refs[n_e : n_e + 2 * count]
        x1_ref, b1_ref, x2_ref, m_ref, out_ref = refs[n_e + 2 * count : n_e + 2 * count + 5]
        even_e, even_s, odd_e, odd_s, packed_e, l_even, le_s, packed_o, l_odd, lo_s = refs[n_e + 2 * count + 5 :]
        le_copy = Whole(named(even_ring, l_refs[:count]), packed_e, le_s, count, True)
        lo_copy = Whole(named(odd_ring, l_refs[count:]), packed_o, lo_s, count, True)
        e_odd = Whole(e_pieces(refs[:n_e], 1), odd_e, odd_s, count)
        e_even = Whole(e_pieces(refs[:n_e], 0), even_e, even_s, count)
        past = lax.axis_index("tm") < 1
        one = jnp.concatenate([x1_ref[...], b1_ref[...]], axis=0)
        two = x2_ref[...]
        le_copy.wait()
        unpack(packed_e, l_even, count)
        near = by_symmetric(one, l_even[...])
        g = offsets_of(packed_e)
        row = nt(g, one)[0:1] + nt(g, two)[1:2]
        v_row = one_row(m_ref[2 * rows :, :rows])
        row = row + jnp.concatenate([jnp.zeros_like(v_row), v_row], axis=1)
        behind = nt(m_ref[rows : 2 * rows, :], e_odd.wait()[...])
        lo_copy.wait()
        unpack(packed_o, l_odd, count)
        far = by_symmetric(two, l_odd[...])
        far = far + jnp.concatenate([jnp.zeros_like(behind), behind], axis=0)
        total = near + nt(far.astype(BF16), e_even.wait()[...])
        out_ref[: 2 * rows, :] = jnp.where(past, 0.0, total).astype(BF16)
        out_ref[2 * rows :, :] = jnp.zeros((TAIL, size), BF16)
        out_ref[2 * rows :, : 2 * rows] = two_rows(jnp.where(past, 0.0, row))

    (m2,) = call(
        fourth,
        e_ins + even_ins + odd_ins + [(x1_in, VMEM), (b1_in, VMEM), (x2, VMEM), (m1_in, VMEM)],
        [message],
        e_space + e_space + [even_packed] + l_space + [odd_packed] + l_space,
        12 * one_product,
    )
    m2_in = hop(m2, "tm", -1)

    def sixth(*refs):
        l_refs = refs[n_e : n_e + 2 * count]
        m1_ref, b4_ref, m2_ref, own, l_own, g_own = refs[n_e + 2 * count : n_e + 2 * count + 6]
        e_out, g_out, l_out = refs[n_e + 2 * count + 6 : n_e + 2 * count + 9]
        even_e, even_s, odd_e, odd_s, packed_e, le_s, packed_o, l_odd, lo_s = refs[n_e + 2 * count + 9 :]
        lo_copy = Whole(named(odd_ring, l_refs[count:]), packed_o, lo_s, count, True)
        le_copy = Whole(named(even_ring, l_refs[:count]), packed_e, le_s, count, True)
        e_odd = Whole(e_pieces(refs[:n_e], 1), odd_e, odd_s, count)
        e_even = Whole(e_pieces(refs[:n_e], 0), even_e, even_s, count)
        e_out[0] = m1_ref[:rows, :]
        e_out[1] = b4_ref[...]
        lo_copy.wait()
        unpack(packed_o, l_odd, count)
        near = by_symmetric(own[0], l_odd[...])
        le_copy.wait()
        row = nt(offsets_of(packed_e), own[0])[1:2]
        back_row = one_row(m2_ref[2 * rows :, : 2 * rows])
        g = g_own[...].astype(F32)
        g_out[0:1, :] = (g[0:1] + row + back_row[:, :rows]).astype(BF16)
        g_out[1:2, :] = (g[1:2] + back_row[:, rows:]).astype(BF16)
        behind = nt(m2_ref[: 2 * rows, :], e_odd.wait()[...])
        l_out[1] = (behind[rows:] + l_own[1].astype(F32)).astype(BF16)
        near = (near + behind[:rows]).astype(BF16)
        l_out[0] = (nt(near, e_even.wait()[...]) + l_own[0].astype(F32)).astype(BF16)

    e_new, g_new, l_new = call(
        sixth,
        e_ins
        + even_ins
        + odd_ins
        + [(m1_in, VMEM), (b4_in, VMEM), (m2_in, VMEM), (trans, VMEM), (spread, VMEM), (offset, VMEM)],
        [(trans.shape, BF16), (offset.shape, BF16), (spread.shape, BF16)],
        e_space
        + e_space
        + [even_packed, pltpu.SemaphoreType.DMA((count,)), odd_packed]
        + l_space,
        6 * one_product,
    )
    return e_new, g_new, l_new


def solution(mesh):
    placed = (P("tm", "row", None), P("tm", "row"), P("tm", "row", None))
    return jax.shard_map(on_device, mesh=mesh, in_specs=placed, out_specs=placed, check_vma=False)
```

```python
import jax
import jax.numpy as jnp
from jax import lax
from jax.experimental import pallas as pl
from jax.experimental.pallas import tpu as pltpu
from jax.sharding import PartitionSpec as P


BF16, F32 = jnp.bfloat16, jnp.float32
HBM = pl.BlockSpec(memory_space=pl.ANY)
VMEM = pl.BlockSpec(memory_space=pltpu.VMEM)
GRANT = 12 * 2**20
TAIL = 16


def hop(block, axis, distance):
    size = lax.axis_size(axis)
    return lax.ppermute(block, axis, [(i, (i + distance) % size) for i in range(size)])


def nn(a, b):
    return lax.dot_general(a, b, (((1,), (0,)), ((), ())), preferred_element_type=F32)


def nt(a, b):
    return lax.dot_general(a, b, (((1,), (1,)), ((), ())), preferred_element_type=F32)


def kept(shape, kind):
    return pltpu.VMEM(shape, kind)


def near(array):
    return pltpu.with_memory_space_constraint(array, pltpu.VMEM)


def call(body, ins, outs, flops, after=()):
    count = len(ins)

    def run(*refs):
        body(*refs[:count], *refs[count + len(after) :])

    return pl.pallas_call(
        run,
        in_specs=[VMEM] * count + [HBM] * len(after),
        out_specs=tuple(VMEM for _ in outs),
        out_shape=tuple(outs),
        cost_estimate=pl.CostEstimate(flops=flops, bytes_accessed=2**20, transcendentals=0),
        compiler_params=pltpu.CompilerParams(vmem_limit_bytes=GRANT),
    )(*[near(array) for array in ins], *after)


def part(array, picked, shape):
    def copy(ref, out):
        out[...] = ref[picked]

    return call(copy, [array], [kept(shape, BF16)], 1000)[0]


def slot(offset, count):
    return lax.rem(lax.axis_index("row") + (offset + count), count)


def join(pieces, whole, count):
    rows = whole.shape[0] // count
    for offset, panel in pieces:
        start = pl.multiple_of(slot(offset, count) * rows, rows)
        whole[pl.ds(start, rows), :] = panel


def unpack(pieces, whole, count):
    size = whole.shape[0] // count
    half = count // 2
    whole[...] = jnp.zeros(whole.shape, BF16)
    for offset, (ref, base) in pieces:
        s = slot(offset, count)
        row = pl.multiple_of(s * size, size)
        for k in range(half):
            column = pl.multiple_of(lax.rem(s + k, count) * size, size)
            whole[pl.ds(row, size), pl.ds(column, size)] = ref[base + k * size : base + (k + 1) * size, :]
        a = lax.rem(s, half)
        row = pl.multiple_of(a * size + lax.div(s, half) * (size // 2), size // 2)
        column = pl.multiple_of((a + half) * size, size)
        start = base + half * size
        whole[pl.ds(row, size // 2), pl.ds(column, size)] = ref[start : start + size // 2, :]


def by_symmetric(a, whole):
    return nn(a, whole) + nt(a, whole)


def two_rows(row):
    high = row.astype(BF16).astype(F32)
    index = lax.broadcasted_iota(jnp.int32, (TAIL, row.shape[1]), 0)
    return jnp.where(index == 0, high, jnp.where(index == 1, row - high, 0.0)).astype(BF16)


def one_row(tile):
    return tile[0:1].astype(F32) + tile[1:2].astype(F32)


def on_device(trans, offset, spread):
    count = lax.axis_size("row")
    _, rows, size = trans.shape
    half = count // 2
    packed = half * rows + rows // 2
    product = 2 * rows * size * size
    panel = kept((rows, size), BF16)
    wide = kept((rows, size), F32)
    pair = kept((2 * rows, size), BF16)
    whole = kept((size, size), BF16)
    short = kept((rows + TAIL, size), BF16)
    long = kept((2 * rows + TAIL, size), BF16)
    line = kept((8, rows), F32)

    def gather(block, parts):
        fore, back = [block], [block]
        for _ in range(half - 1):
            fore.append(hop(fore[-1], "row", 1))
            back.append(hop(back[-1], "row", -1))
        halves = parts[0](fore[-1]), parts[1](back[-1])
        even = hop(halves[0], "row", 1)
        odd = hop(halves[1], "row", -1)
        arrays = [block] + fore[1:] + back[1:]
        offsets = [0] + [-k for k in range(1, half)] + list(range(1, half))
        return arrays, offsets, even, odd, halves

    e_arrays, offsets, e_even_last, e_odd_last, _ = gather(
        trans, (lambda x: part(x, 0, (rows, size)), lambda x: part(x, 1, (rows, size)))
    )
    b1_in = hop(part(trans, 1, (rows, size)), "tm", 1)
    n = len(e_arrays)

    def first(*refs):
        last, out, joined = refs[n], refs[n + 1], refs[n + 2]
        join([(way, ref[1]) for way, ref in zip(offsets, refs)] + [(half, last[...])], joined, count)
        out[...] = nn(refs[0][0], joined[...]).astype(BF16)

    x1, e_odd = call(first, e_arrays + [e_odd_last], [panel, whole], product)
    x1_in = hop(x1, "tm", 1)

    def evens(*refs):
        last, joined = refs[n], refs[n + 1]
        join([(way, ref[0]) for way, ref in zip(offsets, refs)] + [(half, last[...])], joined, count)

    (e_even,) = call(evens, e_arrays + [e_even_last], [whole], 1000)

    def pack(l_ref, g_ref, out):
        z = lax.axis_index("row")
        for b in range(2):
            base = b * (packed + TAIL)
            for k in range(half):
                c = lax.rem(z + k, count)
                tile = l_ref[b, :, pl.ds(pl.multiple_of(c * rows, rows), rows)]
                out[base + k * rows : base + (k + 1) * rows, :] = tile * jnp.asarray(0.5, BF16) if k == 0 else tile
            c = lax.rem(z + half, count)
            tile = l_ref[b, :, pl.ds(pl.multiple_of(c * rows, rows), rows)].astype(F32)
            lower = tile.T[rows // 2 :]
            out[base + half * rows : base + packed, :] = jnp.where(z < half, tile[: rows // 2], lower).astype(BF16)
        g = g_ref[...].astype(F32)
        index = lax.broadcasted_iota(jnp.int32, (TAIL, rows), 0)
        tile = jnp.where(index == 0, g[0:1], jnp.where(index == 1, g[1:2], 0.0))
        out[packed : packed + TAIL, :] = tile.astype(BF16)

    (sent,) = call(
        pack, [spread, offset], [kept((2 * packed + TAIL, rows), BF16)], 1000
    )
    l_arrays, _, l_even_last, l_odd_last, _ = gather(
        sent, (
            lambda x: part(x, slice(0, packed + TAIL), (packed + TAIL, rows)),
            lambda x: part(x, slice(packed + TAIL, 2 * packed + TAIL), (packed, rows)),
        ),
    )

    def second(x1_ref, b1_ref, even, odd, x3_ref, b3_ref, x2_ref):
        past = lax.axis_index("tm") < 1
        one = jnp.concatenate([x1_ref[...], b1_ref[...]], axis=0)
        two = nn(one, even[...]).astype(BF16)
        three = nn(two, odd[...])
        three = jnp.where(past, one.astype(F32), three).astype(BF16)
        x3_ref[...] = three[:rows]
        b3_ref[...] = three[rows:]
        x2_ref[...] = two

    x3, b3, x2 = call(second, [x1_in, b1_in, e_even, e_odd], [panel, panel, pair], 4 * product)
    b3_in = hop(b3, "tm", 1)

    def third(b3_ref, even, b4_ref):
        own = b3_ref[...]
        past = lax.axis_index("tm") < 2
        b4_ref[...] = jnp.where(past, own.astype(F32), nn(own, even[...])).astype(BF16)


    def fourth(*refs):
        last, b3_ref, m_ref, joined, g_ref = refs[n : n + 5]
        unpack([(way, (ref, 0)) for way, ref in zip(offsets, refs)] + [(half, (last, 0))], joined, count)
        for way, ref in list(zip(offsets, refs)) + [(half, last)]:
            column = pl.multiple_of(slot(way, count) * rows, rows)
            g_ref[:, pl.ds(column, rows)] = ref[packed : packed + TAIL, :]
        past = lax.axis_index("tm") < 2
        own = b3_ref[...]
        m_ref[:rows, :] = jnp.where(past, 0.0, by_symmetric(own, joined[...])).astype(BF16)
        m_ref[rows:, :] = jnp.zeros((TAIL, size), BF16)
        m_ref[rows:, :rows] = two_rows(jnp.where(past, 0.0, nt(g_ref[...], own)[0:1]))

    v, l_even, g_all = call(
        fourth, l_arrays + [l_even_last, b3_in], [short, whole, kept((TAIL, size), BF16)], 2 * product
    )
    v_in = hop(v, "tm", -1)
    (b4,) = call(third, [b3_in, e_even], [panel], product, after=(v,))
    b4_in = hop(b4, "tm", -2)

    def fifth(*refs):
        last, x1_ref, b1_ref, x2_ref, x3_ref, even, l_ev, g_ref, own = refs[n : n + 9]
        m_ref, near_ref, far_ref, head_ref, row_ref, l_od = refs[n + 9 :]
        unpack([(way, (ref, packed + TAIL)) for way, ref in zip(offsets, refs)] + [(half, (last, 0))], l_od, count)
        past = lax.axis_index("tm") < 1
        one = jnp.concatenate([x1_ref[...], b1_ref[...]], axis=0)
        two = x2_ref[...]
        close = by_symmetric(one, l_ev[...])
        far = by_symmetric(jnp.concatenate([two, own[0]], axis=0), l_od[...])
        w = close[:rows] + nt(far[:rows].astype(BF16), even[...])
        near_ref[...] = close[rows:]
        far_ref[...] = far[rows : 2 * rows]
        head_ref[...] = far[2 * rows :]
        g = g_ref[...]
        row = nt(g, one)[0:1] + nt(g, two)[1:2]
        index = lax.broadcasted_iota(jnp.int32, (8, rows), 0)
        row_ref[...] = jnp.where(index == 0, row[:, rows:], nt(g, own[0])[1:2])
        m_ref[:rows, :] = jnp.where(past, 0.0, w).astype(BF16)
        m_ref[rows : 2 * rows, :] = x3_ref[...]
        m_ref[2 * rows :, :] = jnp.zeros((TAIL, size), BF16)
        m_ref[2 * rows :, :rows] = two_rows(jnp.where(past, 0.0, row[:, :rows]))

    w, close, far, head, line_, _ = call(
        fifth,
        l_arrays + [l_odd_last, x1_in, b1_in, x2, x3, e_even, l_even, g_all, trans],
        [long, wide, wide, wide, line, whole],
        11 * product,
        after=(v, b4),
    )
    w_in = hop(w, "tm", -1)

    def sixth(v_ref, close_ref, far_ref, line_ref, even, odd, m_ref):
        past = lax.axis_index("tm") < 1
        behind = far_ref[...] + nt(v_ref[:rows, :], odd[...])
        u = close_ref[...] + nt(behind.astype(BF16), even[...])
        row = line_ref[0:1] + one_row(v_ref[rows:, :rows])
        m_ref[:rows, :] = jnp.where(past, 0.0, u).astype(BF16)
        m_ref[rows:, :] = jnp.zeros((TAIL, size), BF16)
        m_ref[rows:, :rows] = two_rows(jnp.where(past, 0.0, row))

    (u,) = call(sixth, [v_in, close, far, line_, e_even, e_odd], [short], 2 * product)
    u_in = hop(u, "tm", -1)

    def seventh(w_ref, head_ref, even, odd, l_own, out):
        inner = head_ref[...] + nt(w_ref[:rows, :], odd[...])
        out[...] = (nt(inner.astype(BF16), even[...]) + l_own[0].astype(F32)).astype(BF16)

    (l_first,) = call(seventh, [w_in, head, e_even, e_odd, spread], [panel], 2 * product, after=(u,))

    def eighth(w_ref, u_ref, b4_ref, line_ref, odd, l_ref, l_own, g_own, e_out, g_out, l_out):
        l_out[1] = (nt(u_ref[:rows, :], odd[...]) + l_own[1].astype(F32)).astype(BF16)
        l_out[0] = l_ref[...]
        e_out[0] = w_ref[rows : 2 * rows, :]
        e_out[1] = b4_ref[...]
        g = g_own[...].astype(F32)
        g_out[0:1, :] = (g[0:1] + line_ref[1:2] + one_row(w_ref[2 * rows :, :rows])).astype(BF16)
        g_out[1:2, :] = (g[1:2] + one_row(u_ref[rows:, :rows])).astype(BF16)

    return call(
        eighth,
        [w_in, u_in, b4_in, line_, e_odd, l_first, spread, offset],
        [jax.ShapeDtypeStruct(x.shape, BF16) for x in (trans, offset, spread)],
        product,
    )


def solution(mesh):
    placed = (P("tm", "row", None), P("tm", "row"), P("tm", "row", None))
    return jax.shard_map(on_device, mesh=mesh, in_specs=placed, out_specs=placed, check_vma=False)
```

```python
import jax
import jax.numpy as jnp
from jax import lax
from jax.experimental import pallas as pl
from jax.experimental.pallas import tpu as pltpu
from jax.sharding import PartitionSpec as P


BF16, F32 = jnp.bfloat16, jnp.float32
HBM = pl.BlockSpec(memory_space=pl.ANY)
VMEM = pl.BlockSpec(memory_space=pltpu.VMEM)
GRANT = 12 * 2**20
TAIL = 16


def hop(block, axis, distance):
    size = lax.axis_size(axis)
    return lax.ppermute(block, axis, [(i, (i + distance) % size) for i in range(size)])


def nn(a, b):
    return lax.dot_general(a, b, (((1,), (0,)), ((), ())), preferred_element_type=F32)


def nt(a, b):
    return lax.dot_general(a, b, (((1,), (1,)), ((), ())), preferred_element_type=F32)


def kept(shape, kind):
    return pltpu.VMEM(shape, kind)


def near(array):
    return pltpu.with_memory_space_constraint(array, pltpu.VMEM)


def apart(array):
    return pltpu.with_memory_space_constraint(array, pltpu.HBM)


def call(body, ins, outs, flops, after=(), wide=(), scratch=()):
    count = len(ins) + len(wide)

    def run(*refs):
        body(*refs[:count], *refs[count + len(after) :])

    return pl.pallas_call(
        run,
        in_specs=[HBM] * len(wide) + [VMEM] * len(ins) + [HBM] * len(after),
        out_specs=tuple(VMEM for _ in outs),
        out_shape=tuple(outs),
        scratch_shapes=scratch,
        cost_estimate=pl.CostEstimate(flops=flops, bytes_accessed=2**20, transcendentals=0),
        compiler_params=pltpu.CompilerParams(vmem_limit_bytes=GRANT),
    )(*[apart(array) for array in wide], *[near(array) for array in ins], *after)


def part(array, picked, shape):
    def copy(ref, out):
        out[...] = ref[picked]

    return call(copy, [array], [kept(shape, BF16)], 1000)[0]


def slot(offset, count):
    return lax.rem(lax.axis_index("row") + (offset + count), count)


def unpack(pieces, whole, count):
    size = whole.shape[0] // count
    half = count // 2
    whole[...] = jnp.zeros(whole.shape, BF16)
    for offset, (ref, base) in pieces:
        s = slot(offset, count)
        row = pl.multiple_of(s * size, size)
        for k in range(half):
            column = pl.multiple_of(lax.rem(s + k, count) * size, size)
            whole[pl.ds(row, size), pl.ds(column, size)] = ref[base + k * size : base + (k + 1) * size, :]
        a = lax.rem(s, half)
        row = pl.multiple_of(a * size + lax.div(s, half) * (size // 2), size // 2)
        column = pl.multiple_of((a + half) * size, size)
        start = base + half * size
        whole[pl.ds(row, size // 2), pl.ds(column, size)] = ref[start : start + size // 2, :]


def by_symmetric(a, whole):
    return nn(a, whole) + nt(a, whole)


def two_rows(row):
    high = row.astype(BF16).astype(F32)
    index = lax.broadcasted_iota(jnp.int32, (TAIL, row.shape[1]), 0)
    return jnp.where(index == 0, high, jnp.where(index == 1, row - high, 0.0)).astype(BF16)


def one_row(tile):
    return tile[0:1].astype(F32) + tile[1:2].astype(F32)


def on_device(trans, offset, spread):
    count = lax.axis_size("row")
    _, rows, size = trans.shape
    half = count // 2
    packed = half * rows + rows // 2
    product = 2 * rows * size * size
    panel = kept((rows, size), BF16)
    wide = kept((rows, size), F32)
    pair = kept((2 * rows, size), BF16)
    whole = kept((size, size), BF16)
    short = kept((rows + TAIL, size), BF16)
    long = kept((2 * rows + TAIL, size), BF16)
    line = kept((8, rows), F32)

    def gather(block, parts):
        fore, back = [block], [block]
        for _ in range(half - 1):
            fore.append(hop(fore[-1], "row", 1))
            back.append(hop(back[-1], "row", -1))
        halves = parts[0](fore[-1]), parts[1](back[-1])
        even = hop(halves[0], "row", 1)
        odd = hop(halves[1], "row", -1)
        arrays = [block] + fore[1:] + back[1:]
        offsets = [0] + [-k for k in range(1, half)] + list(range(1, half))
        return arrays, offsets, even, odd

    e_all = lax.all_gather(trans, "row", axis=1, tiled=True)
    b1_in = hop(part(trans, 1, (rows, size)), "tm", 1)

    def pack(l_ref, g_ref, out):
        z = lax.axis_index("row")
        for b in range(2):
            base = b * (packed + TAIL)
            for k in range(half):
                c = lax.rem(z + k, count)
                tile = l_ref[b, :, pl.ds(pl.multiple_of(c * rows, rows), rows)]
                out[base + k * rows : base + (k + 1) * rows, :] = tile * jnp.asarray(0.5, BF16) if k == 0 else tile
            c = lax.rem(z + half, count)
            tile = l_ref[b, :, pl.ds(pl.multiple_of(c * rows, rows), rows)].astype(F32)
            lower = tile.T[rows // 2 :]
            out[base + half * rows : base + packed, :] = jnp.where(z < half, tile[: rows // 2], lower).astype(BF16)
        g = g_ref[...].astype(F32)
        index = lax.broadcasted_iota(jnp.int32, (TAIL, rows), 0)
        tile = jnp.where(index == 0, g[0:1], jnp.where(index == 1, g[1:2], 0.0))
        out[packed : packed + TAIL, :] = tile.astype(BF16)

    (sent,) = call(pack, [spread, offset], [kept((2 * packed + TAIL, rows), BF16)], 1000)
    l_arrays, offsets, l_even_last, l_odd_last = gather(
        sent,
        (
            lambda x: part(x, slice(0, packed + TAIL), (packed + TAIL, rows)),
            lambda x: part(x, slice(packed + TAIL, 2 * packed + TAIL), (packed, rows)),
        ),
    )
    n = len(l_arrays)

    def opened(*refs):
        even_last, odd_last, b1_ref, own = refs[n : n + 4]
        close_ref, head_ref, line_ref, l_ev, l_od, g_ref = refs[n + 4 :]
        unpack([(way, (ref, 0)) for way, ref in zip(offsets, refs)] + [(half, (even_last, 0))], l_ev, count)
        unpack([(way, (ref, packed + TAIL)) for way, ref in zip(offsets, refs)] + [(half, (odd_last, 0))], l_od, count)
        for way, ref in list(zip(offsets, refs)) + [(half, even_last)]:
            column = pl.multiple_of(slot(way, count) * rows, rows)
            g_ref[:, pl.ds(column, rows)] = ref[packed : packed + TAIL, :]
        g = g_ref[...]
        close_ref[...] = by_symmetric(b1_ref[...], l_ev[...])
        head_ref[...] = by_symmetric(own[0], l_od[...])
        index = lax.broadcasted_iota(jnp.int32, (8, rows), 0)
        line_ref[...] = jnp.where(index == 0, nt(g, b1_ref[...])[0:1], nt(g, own[0])[1:2])

    close, head, line1, l_even, l_odd, g_all = call(
        opened,
        l_arrays + [l_even_last, l_odd_last, b1_in, trans],
        [wide, wide, line, whole, whole, kept((TAIL, size), BF16)],
        4 * product,
    )

    def first(all_ref, own, out, odd, sem):
        copy = pltpu.make_async_copy(all_ref.at[1], odd, sem)
        copy.start()
        copy.wait()
        out[...] = nn(own[0], odd[...]).astype(BF16)

    x1, e_odd = call(
        first, [trans], [panel, whole], product, after=(g_all,), wide=(e_all,), scratch=(pltpu.SemaphoreType.DMA,)
    )
    x1_in = hop(x1, "tm", 1)

    def evens(all_ref, even, sem):
        copy = pltpu.make_async_copy(all_ref.at[0], even, sem)
        copy.start()
        copy.wait()

    (e_even,) = call(evens, [], [whole], 1000, after=(x1,), wide=(e_all,), scratch=(pltpu.SemaphoreType.DMA,))

    def second(x1_ref, b1_ref, even, odd, x3_ref, b3_ref, x2_ref):
        past = lax.axis_index("tm") < 1
        one = jnp.concatenate([x1_ref[...], b1_ref[...]], axis=0)
        two = nn(one, even[...]).astype(BF16)
        three = nn(two, odd[...])
        three = jnp.where(past, one.astype(F32), three).astype(BF16)
        x3_ref[...] = three[:rows]
        b3_ref[...] = three[rows:]
        x2_ref[...] = two

    x3, b3, x2 = call(second, [x1_in, b1_in, e_even, e_odd], [panel, panel, pair], 4 * product)
    b3_in = hop(b3, "tm", 1)

    def third(x1_ref, x2_ref, x3_ref, line_ref, even, l_ev, l_od, g_ref, m_ref, far_ref, row_ref):
        past = lax.axis_index("tm") < 1
        two = x2_ref[...]
        far = by_symmetric(two, l_od[...])
        w = by_symmetric(x1_ref[...], l_ev[...]) + nt(far[:rows].astype(BF16), even[...])
        far_ref[...] = far[rows:]
        row = nt(g_ref[...], two)[1:2]
        row_ref[...] = jnp.broadcast_to(line_ref[0:1] + row[:, rows:], row_ref.shape)
        row = nt(g_ref[...], x1_ref[...])[0:1] + row[:, :rows]
        m_ref[:rows, :] = jnp.where(past, 0.0, w).astype(BF16)
        m_ref[rows : 2 * rows, :] = x3_ref[...]
        m_ref[2 * rows :, :] = jnp.zeros((TAIL, size), BF16)
        m_ref[2 * rows :, :rows] = two_rows(jnp.where(past, 0.0, row))

    w, far, line2 = call(
        third, [x1_in, x2, x3, line1, e_even, l_even, l_odd, g_all], [long, wide, line], 7 * product
    )
    w_in = hop(w, "tm", -1)

    def fourth(b3_ref, l_ev, g_ref, m_ref):
        past = lax.axis_index("tm") < 2
        own = b3_ref[...]
        m_ref[:rows, :] = jnp.where(past, 0.0, by_symmetric(own, l_ev[...])).astype(BF16)
        m_ref[rows:, :] = jnp.zeros((TAIL, size), BF16)
        m_ref[rows:, :rows] = two_rows(jnp.where(past, 0.0, nt(g_ref[...], own)[0:1]))

    (v,) = call(fourth, [b3_in, l_even, g_all], [short], 2 * product, after=(w,))
    v_in = hop(v, "tm", -1)

    def fifth(b3_ref, even, b4_ref):
        own = b3_ref[...]
        past = lax.axis_index("tm") < 2
        b4_ref[...] = jnp.where(past, own.astype(F32), nn(own, even[...])).astype(BF16)

    (b4,) = call(fifth, [b3_in, e_even], [panel], product, after=(v,))
    b4_in = hop(b4, "tm", -2)

    def seventh(w_ref, head_ref, even, odd, l_own, out):
        inner = head_ref[...] + nt(w_ref[:rows, :], odd[...])
        out[...] = (nt(inner.astype(BF16), even[...]) + l_own[0].astype(F32)).astype(BF16)

    (l_first,) = call(seventh, [w_in, head, e_even, e_odd, spread], [panel], 2 * product, after=(b4,))

    def sixth(v_ref, close_ref, far_ref, line_ref, even, odd, m_ref):
        past = lax.axis_index("tm") < 1
        behind = far_ref[...] + nt(v_ref[:rows, :], odd[...])
        u = close_ref[...] + nt(behind.astype(BF16), even[...])
        row = line_ref[0:1] + one_row(v_ref[rows:, :rows])
        m_ref[:rows, :] = jnp.where(past, 0.0, u).astype(BF16)
        m_ref[rows:, :] = jnp.zeros((TAIL, size), BF16)
        m_ref[rows:, :rows] = two_rows(jnp.where(past, 0.0, row))

    (u,) = call(sixth, [v_in, close, far, line2, e_even, e_odd], [short], 2 * product, after=(l_first,))
    u_in = hop(u, "tm", -1)

    def eighth(w_ref, u_ref, b4_ref, line_ref, odd, l_ref, l_own, g_own, e_out, g_out, l_out):
        l_out[1] = (nt(u_ref[:rows, :], odd[...]) + l_own[1].astype(F32)).astype(BF16)
        l_out[0] = l_ref[...]
        e_out[0] = w_ref[rows : 2 * rows, :]
        e_out[1] = b4_ref[...]
        g = g_own[...].astype(F32)
        g_out[0:1, :] = (g[0:1] + line_ref[1:2] + one_row(w_ref[2 * rows :, :rows])).astype(BF16)
        g_out[1:2, :] = (g[1:2] + one_row(u_ref[rows:, :rows])).astype(BF16)

    return call(
        eighth,
        [w_in, u_in, b4_in, line1, e_odd, l_first, spread, offset],
        [jax.ShapeDtypeStruct(x.shape, BF16) for x in (trans, offset, spread)],
        product,
    )


def solution(mesh):
    placed = (P("tm", "row", None), P("tm", "row"), P("tm", "row", None))
    return jax.shard_map(on_device, mesh=mesh, in_specs=placed, out_specs=placed, check_vma=False)
```

```python
import jax
import jax.numpy as jnp
from jax import lax
from jax.experimental import pallas as pl
from jax.experimental.pallas import tpu as pltpu
from jax.sharding import PartitionSpec as P


BF16, F32 = jnp.bfloat16, jnp.float32
HBM = pl.BlockSpec(memory_space=pl.ANY)
VMEM = pl.BlockSpec(memory_space=pltpu.VMEM)
GRANT = 12 * 2**20
TAIL = 16


def hop(block, axis, distance):
    size = lax.axis_size(axis)
    return lax.ppermute(block, axis, [(i, (i + distance) % size) for i in range(size)])


def nn(a, b):
    return lax.dot_general(a, b, (((1,), (0,)), ((), ())), preferred_element_type=F32)


def nt(a, b):
    return lax.dot_general(a, b, (((1,), (1,)), ((), ())), preferred_element_type=F32)


def kept(shape, kind):
    return pltpu.VMEM(shape, kind)


def near(array):
    return pltpu.with_memory_space_constraint(array, pltpu.VMEM)


def call(body, ins, outs, flops, after=()):
    count = len(ins)

    def run(*refs):
        body(*refs[:count], *refs[count + len(after) :])

    return pl.pallas_call(
        run,
        in_specs=[VMEM] * count + [HBM] * len(after),
        out_specs=tuple(VMEM for _ in outs),
        out_shape=tuple(outs),
        cost_estimate=pl.CostEstimate(flops=flops, bytes_accessed=2**20, transcendentals=0),
        compiler_params=pltpu.CompilerParams(vmem_limit_bytes=GRANT),
    )(*[near(array) for array in ins], *after)


def part(array, picked, shape, after=()):
    def copy(ref, out):
        out[...] = ref[picked]

    return call(copy, [array], [kept(shape, BF16)], 1000, after)[0]


def slot(offset, count):
    return lax.rem(lax.axis_index("row") + (offset + count), count)


def join(pieces, whole, count):
    rows = whole.shape[0] // count
    for offset, panel in pieces:
        start = pl.multiple_of(slot(offset, count) * rows, rows)
        whole[pl.ds(start, rows), :] = panel


def unpack(pieces, whole, count):
    size = whole.shape[0] // count
    half = count // 2
    whole[...] = jnp.zeros(whole.shape, BF16)
    for offset, (ref, base) in pieces:
        s = slot(offset, count)
        row = pl.multiple_of(s * size, size)
        for k in range(half):
            column = pl.multiple_of(lax.rem(s + k, count) * size, size)
            whole[pl.ds(row, size), pl.ds(column, size)] = ref[base + k * size : base + (k + 1) * size, :]
        a = lax.rem(s, half)
        row = pl.multiple_of(a * size + lax.div(s, half) * (size // 2), size // 2)
        column = pl.multiple_of((a + half) * size, size)
        start = base + half * size
        whole[pl.ds(row, size // 2), pl.ds(column, size)] = ref[start : start + size // 2, :]


def by_symmetric(a, whole):
    return nn(a, whole) + nt(a, whole)


def two_rows(row):
    high = row.astype(BF16).astype(F32)
    index = lax.broadcasted_iota(jnp.int32, (TAIL, row.shape[1]), 0)
    return jnp.where(index == 0, high, jnp.where(index == 1, row - high, 0.0)).astype(BF16)


def one_row(tile):
    return tile[0:1].astype(F32) + tile[1:2].astype(F32)


def on_device(trans, offset, spread):
    count = lax.axis_size("row")
    _, rows, size = trans.shape
    half = count // 2
    packed = half * rows + rows // 2
    product = 2 * rows * size * size
    panel = kept((rows, size), BF16)
    wide = kept((rows, size), F32)
    pair = kept((2 * rows, size), BF16)
    whole = kept((size, size), BF16)
    short = kept((rows + TAIL, size), BF16)
    long = kept((2 * rows + TAIL, size), BF16)
    line = kept((8, rows), F32)

    def gather(block, parts):
        fore, back = [block], [block]
        for _ in range(half - 1):
            fore.append(hop(fore[-1], "row", 1))
            back.append(hop(back[-1], "row", -1))
        halves = parts[0](fore[-1]), parts[1](back[-1])
        even = hop(halves[0], "row", 1)
        odd = hop(halves[1], "row", -1)
        arrays = [block] + fore[1:] + back[1:]
        offsets = [0] + [-k for k in range(1, half)] + list(range(1, half))
        return arrays, offsets, even, odd, halves

    e_arrays, offsets, e_even_last, e_odd_last, e_halves = gather(
        trans, (lambda x: part(x, 0, (rows, size)), lambda x: part(x, 1, (rows, size)))
    )
    b1_in = hop(part(trans, 1, (rows, size)), "tm", 1)

    def pack(l_ref, g_ref, out):
        z = lax.axis_index("row")
        for b in range(2):
            base = b * (packed + TAIL)
            for k in range(half):
                c = lax.rem(z + k, count)
                tile = l_ref[b, :, pl.ds(pl.multiple_of(c * rows, rows), rows)]
                out[base + k * rows : base + (k + 1) * rows, :] = tile * jnp.asarray(0.5, BF16) if k == 0 else tile
            c = lax.rem(z + half, count)
            tile = l_ref[b, :, pl.ds(pl.multiple_of(c * rows, rows), rows)].astype(F32)
            lower = tile.T[rows // 2 :]
            out[base + half * rows : base + packed, :] = jnp.where(z < half, tile[: rows // 2], lower).astype(BF16)
        g = g_ref[...].astype(F32)
        index = lax.broadcasted_iota(jnp.int32, (TAIL, rows), 0)
        tile = jnp.where(index == 0, g[0:1], jnp.where(index == 1, g[1:2], 0.0))
        out[packed : packed + TAIL, :] = tile.astype(BF16)

    (sent,) = call(pack, [spread, offset], [kept((2 * packed + TAIL, rows), BF16)], 1000)
    l_arrays, _, l_even_last, l_odd_last, _ = gather(
        sent,
        (
            lambda x: part(x, slice(0, packed + TAIL), (packed + TAIL, rows), e_halves),
            lambda x: part(x, slice(packed + TAIL, 2 * packed + TAIL), (packed, rows), e_halves),
        ),
    )
    n = len(l_arrays)

    def first(*refs):
        last, out, joined = refs[n], refs[n + 1], refs[n + 2]
        join([(way, ref[1]) for way, ref in zip(offsets, refs)] + [(half, last[...])], joined, count)
        out[...] = nn(refs[0][0], joined[...]).astype(BF16)

    x1, e_odd = call(first, e_arrays + [e_odd_last], [panel, whole], product)
    x1_in = hop(x1, "tm", 1)

    def evens(*refs):
        last, joined = refs[n], refs[n + 1]
        join([(way, ref[0]) for way, ref in zip(offsets, refs)] + [(half, last[...])], joined, count)

    (e_even,) = call(evens, e_arrays + [e_even_last], [whole], 1000, after=(x1,))

    def opened(*refs):
        even_last, odd_last, b1_ref, own = refs[n : n + 4]
        close_ref, head_ref, line_ref, l_ev, l_od, g_ref = refs[n + 4 :]
        unpack([(way, (ref, 0)) for way, ref in zip(offsets, refs)] + [(half, (even_last, 0))], l_ev, count)
        unpack([(way, (ref, packed + TAIL)) for way, ref in zip(offsets, refs)] + [(half, (odd_last, 0))], l_od, count)
        for way, ref in list(zip(offsets, refs)) + [(half, even_last)]:
            column = pl.multiple_of(slot(way, count) * rows, rows)
            g_ref[:, pl.ds(column, rows)] = ref[packed : packed + TAIL, :]
        g = g_ref[...]
        close_ref[...] = by_symmetric(b1_ref[...], l_ev[...])
        head_ref[...] = by_symmetric(own[0], l_od[...])
        index = lax.broadcasted_iota(jnp.int32, (8, rows), 0)
        line_ref[...] = jnp.where(index == 0, nt(g, b1_ref[...])[0:1], nt(g, own[0])[1:2])

    close, head, line1, l_even, l_odd, g_all = call(
        opened,
        l_arrays + [l_even_last, l_odd_last, b1_in, trans],
        [wide, wide, line, whole, whole, kept((TAIL, size), BF16)],
        4 * product,
        after=(e_even,),
    )

    def second(x1_ref, b1_ref, even, odd, x3_ref, b3_ref, x2_ref):
        past = lax.axis_index("tm") < 1
        one = jnp.concatenate([x1_ref[...], b1_ref[...]], axis=0)
        two = nn(one, even[...]).astype(BF16)
        three = nn(two, odd[...])
        three = jnp.where(past, one.astype(F32), three).astype(BF16)
        x3_ref[...] = three[:rows]
        b3_ref[...] = three[rows:]
        x2_ref[...] = two

    x3, b3, x2 = call(second, [x1_in, b1_in, e_even, e_odd], [panel, panel, pair], 4 * product, after=(g_all,))
    b3_in = hop(b3, "tm", 1)

    def third(x1_ref, x2_ref, x3_ref, line_ref, even, l_ev, l_od, g_ref, m_ref, far_ref, row_ref):
        past = lax.axis_index("tm") < 1
        two = x2_ref[...]
        far = by_symmetric(two, l_od[...])
        w = by_symmetric(x1_ref[...], l_ev[...]) + nt(far[:rows].astype(BF16), even[...])
        far_ref[...] = far[rows:]
        row = nt(g_ref[...], two)[1:2]
        row_ref[...] = jnp.broadcast_to(line_ref[0:1] + row[:, rows:], row_ref.shape)
        row = nt(g_ref[...], x1_ref[...])[0:1] + row[:, :rows]
        m_ref[:rows, :] = jnp.where(past, 0.0, w).astype(BF16)
        m_ref[rows : 2 * rows, :] = x3_ref[...]
        m_ref[2 * rows :, :] = jnp.zeros((TAIL, size), BF16)
        m_ref[2 * rows :, :rows] = two_rows(jnp.where(past, 0.0, row))

    w, far, line2 = call(
        third, [x1_in, x2, x3, line1, e_even, l_even, l_odd, g_all], [long, wide, line], 7 * product
    )
    w_in = hop(w, "tm", -1)

    def fourth(b3_ref, l_ev, g_ref, m_ref):
        past = lax.axis_index("tm") < 2
        own = b3_ref[...]
        m_ref[:rows, :] = jnp.where(past, 0.0, by_symmetric(own, l_ev[...])).astype(BF16)
        m_ref[rows:, :] = jnp.zeros((TAIL, size), BF16)
        m_ref[rows:, :rows] = two_rows(jnp.where(past, 0.0, nt(g_ref[...], own)[0:1]))

    (v,) = call(fourth, [b3_in, l_even, g_all], [short], 2 * product, after=(w,))
    v_in = hop(v, "tm", -1)

    def fifth(b3_ref, even, b4_ref):
        own = b3_ref[...]
        past = lax.axis_index("tm") < 2
        b4_ref[...] = jnp.where(past, own.astype(F32), nn(own, even[...])).astype(BF16)

    (b4,) = call(fifth, [b3_in, e_even], [panel], product, after=(v,))
    b4_in = hop(b4, "tm", -2)

    def sixth(v_ref, close_ref, far_ref, line_ref, even, odd, m_ref):
        past = lax.axis_index("tm") < 1
        behind = far_ref[...] + nt(v_ref[:rows, :], odd[...])
        u = close_ref[...] + nt(behind.astype(BF16), even[...])
        row = line_ref[0:1] + one_row(v_ref[rows:, :rows])
        m_ref[:rows, :] = jnp.where(past, 0.0, u).astype(BF16)
        m_ref[rows:, :] = jnp.zeros((TAIL, size), BF16)
        m_ref[rows:, :rows] = two_rows(jnp.where(past, 0.0, row))

    (u,) = call(sixth, [v_in, close, far, line2, e_even, e_odd], [short], 2 * product, after=(b4,))
    u_in = hop(u, "tm", -1)

    def seventh(w_ref, head_ref, even, odd, l_own, out):
        inner = head_ref[...] + nt(w_ref[:rows, :], odd[...])
        out[...] = (nt(inner.astype(BF16), even[...]) + l_own[0].astype(F32)).astype(BF16)

    (l_first,) = call(seventh, [w_in, head, e_even, e_odd, spread], [panel], 2 * product, after=(u,))

    def eighth(w_ref, u_ref, b4_ref, line_ref, odd, l_ref, l_own, g_own, e_out, g_out, l_out):
        l_out[1] = (nt(u_ref[:rows, :], odd[...]) + l_own[1].astype(F32)).astype(BF16)
        l_out[0] = l_ref[...]
        e_out[0] = w_ref[rows : 2 * rows, :]
        e_out[1] = b4_ref[...]
        g = g_own[...].astype(F32)
        g_out[0:1, :] = (g[0:1] + line_ref[1:2] + one_row(w_ref[2 * rows :, :rows])).astype(BF16)
        g_out[1:2, :] = (g[1:2] + one_row(u_ref[rows:, :rows])).astype(BF16)

    return call(
        eighth,
        [w_in, u_in, b4_in, line1, e_odd, l_first, spread, offset],
        [jax.ShapeDtypeStruct(x.shape, BF16) for x in (trans, offset, spread)],
        product,
    )


def solution(mesh):
    placed = (P("tm", "row", None), P("tm", "row"), P("tm", "row", None))
    return jax.shard_map(on_device, mesh=mesh, in_specs=placed, out_specs=placed, check_vma=False)
```

```python
import jax
import jax.numpy as jnp
from jax import lax
from jax.experimental import pallas as pl
from jax.experimental.pallas import tpu as pltpu
from jax.sharding import PartitionSpec as P


BF16, F32 = jnp.bfloat16, jnp.float32
HBM = pl.BlockSpec(memory_space=pl.ANY)
VMEM = pl.BlockSpec(memory_space=pltpu.VMEM)
GRANT = 12 * 2**20
TAIL = 16


def hop(block, axis, distance):
    size = lax.axis_size(axis)
    return lax.ppermute(block, axis, [(i, (i + distance) % size) for i in range(size)])


def nn(a, b):
    return lax.dot_general(a, b, (((1,), (0,)), ((), ())), preferred_element_type=F32)


def nt(a, b):
    return lax.dot_general(a, b, (((1,), (1,)), ((), ())), preferred_element_type=F32)


def kept(shape, kind):
    return pltpu.VMEM(shape, kind)


def near(array):
    return pltpu.with_memory_space_constraint(array, pltpu.VMEM)


def call(body, ins, outs, flops, after=()):
    count = len(ins)

    def run(*refs):
        body(*refs[:count], *refs[count + len(after) :])

    return pl.pallas_call(
        run,
        in_specs=[VMEM] * count + [HBM] * len(after),
        out_specs=tuple(VMEM for _ in outs),
        out_shape=tuple(outs),
        cost_estimate=pl.CostEstimate(flops=flops, bytes_accessed=2**20, transcendentals=0),
        compiler_params=pltpu.CompilerParams(vmem_limit_bytes=GRANT),
    )(*[near(array) for array in ins], *after)


def part(array, picked, shape, after=()):
    def copy(ref, out):
        out[...] = ref[picked]

    return call(copy, [array], [kept(shape, BF16)], 1000, after)[0]


def slot(offset, count):
    return lax.rem(lax.axis_index("row") + (offset + count), count)


def join(pieces, whole, count):
    rows = whole.shape[0] // count
    for offset, panel in pieces:
        start = pl.multiple_of(slot(offset, count) * rows, rows)
        whole[pl.ds(start, rows), :] = panel


def unpack(pieces, whole, count):
    size = whole.shape[0] // count
    half = count // 2
    whole[...] = jnp.zeros(whole.shape, BF16)
    for offset, (ref, base) in pieces:
        s = slot(offset, count)
        row = pl.multiple_of(s * size, size)
        for k in range(half):
            column = pl.multiple_of(lax.rem(s + k, count) * size, size)
            whole[pl.ds(row, size), pl.ds(column, size)] = ref[base + k * size : base + (k + 1) * size, :]
        a = lax.rem(s, half)
        row = pl.multiple_of(a * size + lax.div(s, half) * (size // 2), size // 2)
        column = pl.multiple_of((a + half) * size, size)
        start = base + half * size
        whole[pl.ds(row, size // 2), pl.ds(column, size)] = ref[start : start + size // 2, :]


def by_symmetric(a, whole):
    return nn(a, whole) + nt(a, whole)


def two_rows(row):
    high = row.astype(BF16).astype(F32)
    index = lax.broadcasted_iota(jnp.int32, (TAIL, row.shape[1]), 0)
    return jnp.where(index == 0, high, jnp.where(index == 1, row - high, 0.0)).astype(BF16)


def one_row(tile):
    return tile[0:1].astype(F32) + tile[1:2].astype(F32)


def on_device(trans, offset, spread):
    count = lax.axis_size("row")
    _, rows, size = trans.shape
    half = count // 2
    packed = half * rows + rows // 2
    product = 2 * rows * size * size
    panel = kept((rows, size), BF16)
    wide = kept((rows, size), F32)
    pair = kept((2 * rows, size), BF16)
    whole = kept((size, size), BF16)
    short = kept((rows + TAIL, size), BF16)
    long = kept((2 * rows + TAIL, size), BF16)
    line = kept((8, rows), F32)

    def gather(block, parts):
        fore, back = [block], [block]
        for _ in range(half - 1):
            fore.append(hop(fore[-1], "row", 1))
            back.append(hop(back[-1], "row", -1))
        halves = parts[0](fore[-1]), parts[1](back[-1])
        even = hop(halves[0], "row", 1)
        odd = hop(halves[1], "row", -1)
        arrays = [block] + fore[1:] + back[1:]
        offsets = [0] + [-k for k in range(1, half)] + list(range(1, half))
        return arrays, offsets, even, odd, halves

    e_arrays, offsets, e_even_last, e_odd_last, e_halves = gather(
        trans, (lambda x: part(x, 0, (rows, size)), lambda x: part(x, 1, (rows, size)))
    )
    b1_in = hop(part(trans, 1, (rows, size)), "tm", 1)

    def pack(l_ref, g_ref, out):
        z = lax.axis_index("row")
        for b in range(2):
            base = b * (packed + TAIL)
            for k in range(half):
                c = lax.rem(z + k, count)
                tile = l_ref[b, :, pl.ds(pl.multiple_of(c * rows, rows), rows)]
                out[base + k * rows : base + (k + 1) * rows, :] = tile * jnp.asarray(0.5, BF16) if k == 0 else tile
            c = lax.rem(z + half, count)
            tile = l_ref[b, :, pl.ds(pl.multiple_of(c * rows, rows), rows)].astype(F32)
            lower = tile.T[rows // 2 :]
            out[base + half * rows : base + packed, :] = jnp.where(z < half, tile[: rows // 2], lower).astype(BF16)
        g = g_ref[...].astype(F32)
        index = lax.broadcasted_iota(jnp.int32, (TAIL, rows), 0)
        tile = jnp.where(index == 0, g[0:1], jnp.where(index == 1, g[1:2], 0.0))
        out[packed : packed + TAIL, :] = tile.astype(BF16)

    (sent,) = call(pack, [spread, offset], [kept((2 * packed + TAIL, rows), BF16)], 1000)
    l_arrays, _, l_even_last, l_odd_last, _ = gather(
        sent,
        (
            lambda x: part(x, slice(0, packed + TAIL), (packed + TAIL, rows), e_halves),
            lambda x: part(x, slice(packed + TAIL, 2 * packed + TAIL), (packed, rows), e_halves),
        ),
    )
    n = len(l_arrays)

    def first(*refs):
        even_last, odd_last, b1_ref, out, b2_ref, even, odd = refs[n:]
        past = lax.axis_index("tm") < 1
        join([(way, ref[0]) for way, ref in zip(offsets, refs)] + [(half, even_last[...])], even, count)
        b1 = b1_ref[...]
        b2 = nn(b1, even[...]).astype(BF16)
        b2_ref[...] = b2
        join([(way, ref[1]) for way, ref in zip(offsets, refs)] + [(half, odd_last[...])], odd, count)
        both = nn(jnp.concatenate([refs[0][0], b2], axis=0), odd[...])
        out[:rows, :] = both[:rows].astype(BF16)
        out[rows:, :] = jnp.where(past, b1.astype(F32), both[rows:]).astype(BF16)

    m, b2, e_even, e_odd = call(
        first, e_arrays + [e_even_last, e_odd_last, b1_in], [pair, panel, whole, whole], 3 * product
    )
    m_in = hop(m, "tm", 1)

    def opened(*refs):
        even_last, odd_last, b1_ref, b2_ref, own = refs[n : n + 5]
        close_ref, far_ref, head_ref, line_ref, l_ev, l_od, g_ref = refs[n + 5 :]
        unpack([(way, (ref, 0)) for way, ref in zip(offsets, refs)] + [(half, (even_last, 0))], l_ev, count)
        unpack([(way, (ref, packed + TAIL)) for way, ref in zip(offsets, refs)] + [(half, (odd_last, 0))], l_od, count)
        for way, ref in list(zip(offsets, refs)) + [(half, even_last)]:
            column = pl.multiple_of(slot(way, count) * rows, rows)
            g_ref[:, pl.ds(column, rows)] = ref[packed : packed + TAIL, :]
        g = g_ref[...]
        close_ref[...] = by_symmetric(b1_ref[...], l_ev[...])
        far = by_symmetric(jnp.concatenate([own[0], b2_ref[...]], axis=0), l_od[...])
        head_ref[...] = far[:rows]
        far_ref[...] = far[rows:]
        index = lax.broadcasted_iota(jnp.int32, (8, rows), 0)
        row = nt(g, b1_ref[...])[0:1] + nt(g, b2_ref[...])[1:2]
        line_ref[...] = jnp.where(index == 0, row, nt(g, own[0])[1:2])

    close, far, head, line_, l_even, l_odd, g_all = call(
        opened,
        l_arrays + [l_even_last, l_odd_last, b1_in, b2, trans],
        [wide, wide, wide, line, whole, whole, kept((TAIL, size), BF16)],
        6 * product,
        after=(m,),
    )

    def fourth(m_ref, l_ev, g_ref, out):
        past = lax.axis_index("tm") < 2
        own = m_ref[rows:, :]
        out[:rows, :] = jnp.where(past, 0.0, by_symmetric(own, l_ev[...])).astype(BF16)
        out[rows:, :] = jnp.zeros((TAIL, size), BF16)
        out[rows:, :rows] = two_rows(jnp.where(past, 0.0, nt(g_ref[...], own)[0:1]))

    (v,) = call(fourth, [m_in, l_even, g_all], [short], 2 * product)
    v_in = hop(v, "tm", -1)

    def third(m_ref, even, odd, l_ev, l_od, g_ref, out):
        past = lax.axis_index("tm") < 1
        one = m_ref[:rows, :]
        two = nn(one, even[...]).astype(BF16)
        three = jnp.where(past, one.astype(F32), nn(two, odd[...]))
        far = by_symmetric(two, l_od[...])
        w = by_symmetric(one, l_ev[...]) + nt(far.astype(BF16), even[...])
        row = nt(g_ref[...], one)[0:1] + nt(g_ref[...], two)[1:2]
        out[:rows, :] = jnp.where(past, 0.0, w).astype(BF16)
        out[rows : 2 * rows, :] = three.astype(BF16)
        out[2 * rows :, :] = jnp.zeros((TAIL, size), BF16)
        out[2 * rows :, :rows] = two_rows(jnp.where(past, 0.0, row))

    (w,) = call(third, [m_in, e_even, e_odd, l_even, l_odd, g_all], [long], 7 * product, after=(v,))
    w_in = hop(w, "tm", -1)

    def fifth(m_ref, even, b4_ref):
        own = m_ref[rows:, :]
        past = lax.axis_index("tm") < 2
        b4_ref[...] = jnp.where(past, own.astype(F32), nn(own, even[...])).astype(BF16)

    (b4,) = call(fifth, [m_in, e_even], [panel], product, after=(w,))
    b4_in = hop(b4, "tm", -2)

    def sixth(v_ref, close_ref, far_ref, line_ref, even, odd, m_ref):
        past = lax.axis_index("tm") < 1
        behind = far_ref[...] + nt(v_ref[:rows, :], odd[...])
        u = close_ref[...] + nt(behind.astype(BF16), even[...])
        row = line_ref[0:1] + one_row(v_ref[rows:, :rows])
        m_ref[:rows, :] = jnp.where(past, 0.0, u).astype(BF16)
        m_ref[rows:, :] = jnp.zeros((TAIL, size), BF16)
        m_ref[rows:, :rows] = two_rows(jnp.where(past, 0.0, row))

    (u,) = call(sixth, [v_in, close, far, line_, e_even, e_odd], [short], 2 * product, after=(b4,))
    u_in = hop(u, "tm", -1)

    def seventh(w_ref, head_ref, even, odd, l_own, out):
        inner = head_ref[...] + nt(w_ref[:rows, :], odd[...])
        out[...] = (nt(inner.astype(BF16), even[...]) + l_own[0].astype(F32)).astype(BF16)

    (l_first,) = call(seventh, [w_in, head, e_even, e_odd, spread], [panel], 2 * product, after=(u,))

    def eighth(w_ref, u_ref, b4_ref, line_ref, odd, l_ref, l_own, g_own, e_out, g_out, l_out):
        l_out[1] = (nt(u_ref[:rows, :], odd[...]) + l_own[1].astype(F32)).astype(BF16)
        l_out[0] = l_ref[...]
        e_out[0] = w_ref[rows : 2 * rows, :]
        e_out[1] = b4_ref[...]
        g = g_own[...].astype(F32)
        g_out[0:1, :] = (g[0:1] + line_ref[1:2] + one_row(w_ref[2 * rows :, :rows])).astype(BF16)
        g_out[1:2, :] = (g[1:2] + one_row(u_ref[rows:, :rows])).astype(BF16)

    return call(
        eighth,
        [w_in, u_in, b4_in, line_, e_odd, l_first, spread, offset],
        [jax.ShapeDtypeStruct(x.shape, BF16) for x in (trans, offset, spread)],
        product,
    )


def solution(mesh):
    placed = (P("tm", "row", None), P("tm", "row"), P("tm", "row", None))
    return jax.shard_map(on_device, mesh=mesh, in_specs=placed, out_specs=placed, check_vma=False)
```

```python
import jax
import jax.numpy as jnp
from jax import lax
from jax.experimental import pallas as pl
from jax.experimental.pallas import tpu as pltpu
from jax.sharding import PartitionSpec as P


BF16, F32 = jnp.bfloat16, jnp.float32
HBM = pl.BlockSpec(memory_space=pl.ANY)
VMEM = pl.BlockSpec(memory_space=pltpu.VMEM)
GRANT = 12 * 2**20
TAIL = 16


def hop(block, axis, distance):
    size = lax.axis_size(axis)
    return lax.ppermute(block, axis, [(i, (i + distance) % size) for i in range(size)])


def nn(a, b):
    return lax.dot_general(a, b, (((1,), (0,)), ((), ())), preferred_element_type=F32)


def nt(a, b):
    return lax.dot_general(a, b, (((1,), (1,)), ((), ())), preferred_element_type=F32)


def kept(shape, kind):
    return pltpu.VMEM(shape, kind)


def near(array):
    return pltpu.with_memory_space_constraint(array, pltpu.VMEM)


def call(body, ins, outs, flops, after=()):
    count = len(ins)

    def run(*refs):
        body(*refs[:count], *refs[count + len(after) :])

    return pl.pallas_call(
        run,
        in_specs=[VMEM] * count + [HBM] * len(after),
        out_specs=tuple(VMEM for _ in outs),
        out_shape=tuple(outs),
        cost_estimate=pl.CostEstimate(flops=flops, bytes_accessed=2**20, transcendentals=0),
        compiler_params=pltpu.CompilerParams(vmem_limit_bytes=GRANT),
    )(*[near(array) for array in ins], *after)


def part(array, picked, shape, after=()):
    def copy(ref, out):
        out[...] = ref[picked]

    return call(copy, [array], [kept(shape, BF16)], 1000, after)[0]


def slot(offset, count):
    return lax.rem(lax.axis_index("row") + (offset + count), count)


def join(pieces, whole, count):
    rows = whole.shape[0] // count
    for offset, panel in pieces:
        start = pl.multiple_of(slot(offset, count) * rows, rows)
        whole[pl.ds(start, rows), :] = panel


def unpack(pieces, whole, count):
    size = whole.shape[0] // count
    half = count // 2
    whole[...] = jnp.zeros(whole.shape, BF16)
    for offset, (ref, base) in pieces:
        s = slot(offset, count)
        row = pl.multiple_of(s * size, size)
        for k in range(half):
            column = pl.multiple_of(lax.rem(s + k, count) * size, size)
            whole[pl.ds(row, size), pl.ds(column, size)] = ref[base + k * size : base + (k + 1) * size, :]
        a = lax.rem(s, half)
        row = pl.multiple_of(a * size + lax.div(s, half) * (size // 2), size // 2)
        column = pl.multiple_of((a + half) * size, size)
        start = base + half * size
        whole[pl.ds(row, size // 2), pl.ds(column, size)] = ref[start : start + size // 2, :]


def by_symmetric(a, whole):
    return nn(a, whole) + nt(a, whole)


def two_rows(row):
    high = row.astype(BF16).astype(F32)
    index = lax.broadcasted_iota(jnp.int32, (TAIL, row.shape[1]), 0)
    return jnp.where(index == 0, high, jnp.where(index == 1, row - high, 0.0)).astype(BF16)


def one_row(tile):
    return tile[0:1].astype(F32) + tile[1:2].astype(F32)


def on_device(trans, offset, spread):
    count = lax.axis_size("row")
    _, rows, size = trans.shape
    half = count // 2
    packed = half * rows + rows // 2
    product = 2 * rows * size * size
    panel = kept((rows, size), BF16)
    wide = kept((rows, size), F32)
    pair = kept((2 * rows, size), BF16)
    whole = kept((size, size), BF16)
    short = kept((rows + TAIL, size), BF16)
    long = kept((2 * rows + TAIL, size), BF16)
    line = kept((8, rows), F32)

    def gather(block, parts):
        fore, back = [block], [block]
        for _ in range(half - 1):
            fore.append(hop(fore[-1], "row", 1))
            back.append(hop(back[-1], "row", -1))
        halves = parts[0](fore[-1]), parts[1](back[-1])
        even = hop(halves[0], "row", 1)
        odd = hop(halves[1], "row", -1)
        arrays = [block] + fore[1:] + back[1:]
        offsets = [0] + [-k for k in range(1, half)] + list(range(1, half))
        return arrays, offsets, even, odd, halves

    e_arrays, offsets, e_even_last, e_odd_last, e_halves = gather(
        trans, (lambda x: part(x, 0, (rows, size)), lambda x: part(x, 1, (rows, size)))
    )
    b1_in = hop(part(trans, 1, (rows, size)), "tm", 1)

    def pack(l_ref, g_ref, out):
        z = lax.axis_index("row")
        for b in range(2):
            base = b * (packed + TAIL)
            for k in range(half):
                c = lax.rem(z + k, count)
                tile = l_ref[b, :, pl.ds(pl.multiple_of(c * rows, rows), rows)]
                out[base + k * rows : base + (k + 1) * rows, :] = tile * jnp.asarray(0.5, BF16) if k == 0 else tile
            c = lax.rem(z + half, count)
            tile = l_ref[b, :, pl.ds(pl.multiple_of(c * rows, rows), rows)].astype(F32)
            lower = tile.T[rows // 2 :]
            out[base + half * rows : base + packed, :] = jnp.where(z < half, tile[: rows // 2], lower).astype(BF16)
        g = g_ref[...].astype(F32)
        index = lax.broadcasted_iota(jnp.int32, (TAIL, rows), 0)
        tile = jnp.where(index == 0, g[0:1], jnp.where(index == 1, g[1:2], 0.0))
        out[packed : packed + TAIL, :] = tile.astype(BF16)

    (sent,) = call(pack, [spread, offset], [kept((2 * packed + TAIL, rows), BF16)], 1000)
    l_arrays, _, l_even_last, l_odd_last, _ = gather(
        sent,
        (
            lambda x: part(x, slice(0, packed + TAIL), (packed + TAIL, rows), e_halves),
            lambda x: part(x, slice(packed + TAIL, 2 * packed + TAIL), (packed, rows), e_halves),
        ),
    )
    n = len(l_arrays)

    def first(*refs):
        even_last, odd_last, b1_ref, out, b2_ref, even, odd = refs[n:]
        past = lax.axis_index("tm") < 1
        join([(way, ref[0]) for way, ref in zip(offsets, refs)] + [(half, even_last[...])], even, count)
        b1 = b1_ref[...]
        b2 = nn(b1, even[...]).astype(BF16)
        b2_ref[...] = b2
        join([(way, ref[1]) for way, ref in zip(offsets, refs)] + [(half, odd_last[...])], odd, count)
        both = nn(jnp.concatenate([refs[0][0], b2], axis=0), odd[...])
        out[:rows, :] = both[:rows].astype(BF16)
        out[rows:, :] = jnp.where(past, b1.astype(F32), both[rows:]).astype(BF16)

    m, b2, e_even, e_odd = call(
        first, e_arrays + [e_even_last, e_odd_last, b1_in], [pair, panel, whole, whole], 3 * product
    )
    m_in = hop(m, "tm", 1)

    def opened(*refs):
        last, b1_ref = refs[n : n + 2]
        close_ref, l_ev, g_ref = refs[n + 2 :]
        unpack([(way, (ref, 0)) for way, ref in zip(offsets, refs)] + [(half, (last, 0))], l_ev, count)
        for way, ref in list(zip(offsets, refs)) + [(half, last)]:
            column = pl.multiple_of(slot(way, count) * rows, rows)
            g_ref[:, pl.ds(column, rows)] = ref[packed : packed + TAIL, :]
        close_ref[...] = by_symmetric(b1_ref[...], l_ev[...])

    close, l_even, g_all = call(
        opened,
        l_arrays + [l_even_last, b1_in],
        [wide, whole, kept((TAIL, size), BF16)],
        2 * product,
        after=(m,),
    )

    def fourth(m_ref, l_ev, g_ref, out):
        past = lax.axis_index("tm") < 2
        own = m_ref[rows:, :]
        out[:rows, :] = jnp.where(past, 0.0, by_symmetric(own, l_ev[...])).astype(BF16)
        out[rows:, :] = jnp.zeros((TAIL, size), BF16)
        out[rows:, :rows] = two_rows(jnp.where(past, 0.0, nt(g_ref[...], own)[0:1]))

    (v,) = call(fourth, [m_in, l_even, g_all], [short], 2 * product)
    v_in = hop(v, "tm", -1)

    def odds(*refs):
        last, b1_ref, b2_ref, own, g_ref = refs[n : n + 5]
        far_ref, head_ref, line_ref, l_od = refs[n + 5 :]
        unpack([(way, (ref, packed + TAIL)) for way, ref in zip(offsets, refs)] + [(half, (last, 0))], l_od, count)
        g = g_ref[...]
        far = by_symmetric(jnp.concatenate([own[0], b2_ref[...]], axis=0), l_od[...])
        head_ref[...] = far[:rows]
        far_ref[...] = far[rows:]
        index = lax.broadcasted_iota(jnp.int32, (8, rows), 0)
        row = nt(g, b1_ref[...])[0:1] + nt(g, b2_ref[...])[1:2]
        line_ref[...] = jnp.where(index == 0, row, nt(g, own[0])[1:2])

    far, head, line_, l_odd = call(
        odds,
        l_arrays + [l_odd_last, b1_in, b2, trans, g_all],
        [wide, wide, line, whole],
        4 * product,
        after=(v,),
    )

    def third(m_ref, even, odd, l_ev, l_od, g_ref, out):
        past = lax.axis_index("tm") < 1
        one = m_ref[:rows, :]
        two = nn(one, even[...]).astype(BF16)
        three = jnp.where(past, one.astype(F32), nn(two, odd[...]))
        far = by_symmetric(two, l_od[...])
        w = by_symmetric(one, l_ev[...]) + nt(far.astype(BF16), even[...])
        row = nt(g_ref[...], one)[0:1] + nt(g_ref[...], two)[1:2]
        out[:rows, :] = jnp.where(past, 0.0, w).astype(BF16)
        out[rows : 2 * rows, :] = three.astype(BF16)
        out[2 * rows :, :] = jnp.zeros((TAIL, size), BF16)
        out[2 * rows :, :rows] = two_rows(jnp.where(past, 0.0, row))

    (w,) = call(third, [m_in, e_even, e_odd, l_even, l_odd, g_all], [long], 7 * product, after=(v,))
    w_in = hop(w, "tm", -1)

    def sixth(v_ref, close_ref, far_ref, line_ref, even, odd, m_ref):
        past = lax.axis_index("tm") < 1
        behind = far_ref[...] + nt(v_ref[:rows, :], odd[...])
        u = close_ref[...] + nt(behind.astype(BF16), even[...])
        row = line_ref[0:1] + one_row(v_ref[rows:, :rows])
        m_ref[:rows, :] = jnp.where(past, 0.0, u).astype(BF16)
        m_ref[rows:, :] = jnp.zeros((TAIL, size), BF16)
        m_ref[rows:, :rows] = two_rows(jnp.where(past, 0.0, row))

    (u,) = call(sixth, [v_in, close, far, line_, e_even, e_odd], [short], 2 * product, after=(w,))
    u_in = hop(u, "tm", -1)

    def fifth(m_ref, even, b4_ref):
        own = m_ref[rows:, :]
        past = lax.axis_index("tm") < 2
        b4_ref[...] = jnp.where(past, own.astype(F32), nn(own, even[...])).astype(BF16)

    (b4,) = call(fifth, [m_in, e_even], [panel], product, after=(u,))
    b4_in = hop(b4, "tm", -2)

    def seventh(w_ref, head_ref, even, odd, l_own, out):
        inner = head_ref[...] + nt(w_ref[:rows, :], odd[...])
        out[...] = (nt(inner.astype(BF16), even[...]) + l_own[0].astype(F32)).astype(BF16)

    (l_first,) = call(seventh, [w_in, head, e_even, e_odd, spread], [panel], 2 * product, after=(b4,))

    def eighth(w_ref, u_ref, b4_ref, line_ref, odd, l_ref, l_own, g_own, e_out, g_out, l_out):
        l_out[1] = (nt(u_ref[:rows, :], odd[...]) + l_own[1].astype(F32)).astype(BF16)
        l_out[0] = l_ref[...]
        e_out[0] = w_ref[rows : 2 * rows, :]
        e_out[1] = b4_ref[...]
        g = g_own[...].astype(F32)
        g_out[0:1, :] = (g[0:1] + line_ref[1:2] + one_row(w_ref[2 * rows :, :rows])).astype(BF16)
        g_out[1:2, :] = (g[1:2] + one_row(u_ref[rows:, :rows])).astype(BF16)

    return call(
        eighth,
        [w_in, u_in, b4_in, line_, e_odd, l_first, spread, offset],
        [jax.ShapeDtypeStruct(x.shape, BF16) for x in (trans, offset, spread)],
        product,
    )


def solution(mesh):
    placed = (P("tm", "row", None), P("tm", "row"), P("tm", "row", None))
    return jax.shard_map(on_device, mesh=mesh, in_specs=placed, out_specs=placed, check_vma=False)
```

```python
import jax
import jax.numpy as jnp
from jax import lax
from jax.experimental import pallas as pl
from jax.experimental.pallas import tpu as pltpu
from jax.sharding import PartitionSpec as P


BF16, F32 = jnp.bfloat16, jnp.float32
HBM = pl.BlockSpec(memory_space=pl.ANY)
VMEM = pl.BlockSpec(memory_space=pltpu.VMEM)
GRANT = 12 * 2**20
TAIL = 16


def hop(block, axis, distance):
    size = lax.axis_size(axis)
    return lax.ppermute(block, axis, [(i, (i + distance) % size) for i in range(size)])


def nn(a, b):
    return lax.dot_general(a, b, (((1,), (0,)), ((), ())), preferred_element_type=F32)


def nt(a, b):
    return lax.dot_general(a, b, (((1,), (1,)), ((), ())), preferred_element_type=F32)


def kept(shape, kind):
    return pltpu.VMEM(shape, kind)


def near(array):
    return pltpu.with_memory_space_constraint(array, pltpu.VMEM)


def call(body, ins, outs, flops, after=()):
    count = len(ins)

    def run(*refs):
        body(*refs[:count], *refs[count + len(after) :])

    return pl.pallas_call(
        run,
        in_specs=[VMEM] * count + [HBM] * len(after),
        out_specs=tuple(VMEM for _ in outs),
        out_shape=tuple(outs),
        cost_estimate=pl.CostEstimate(flops=flops, bytes_accessed=2**20, transcendentals=0),
        compiler_params=pltpu.CompilerParams(vmem_limit_bytes=GRANT),
    )(*[near(array) for array in ins], *after)


def part(array, picked, shape, after=()):
    def copy(ref, out):
        out[...] = ref[picked]

    return call(copy, [array], [kept(shape, BF16)], 1000, after)[0]


def slot(offset, count):
    return lax.rem(lax.axis_index("row") + (offset + count), count)


def join(pieces, whole, count):
    rows = whole.shape[0] // count
    for offset, panel in pieces:
        start = pl.multiple_of(slot(offset, count) * rows, rows)
        whole[pl.ds(start, rows), :] = panel


def unpack(pieces, whole, count):
    size = whole.shape[0] // count
    half = count // 2
    whole[...] = jnp.zeros(whole.shape, BF16)
    for offset, (ref, base) in pieces:
        s = slot(offset, count)
        row = pl.multiple_of(s * size, size)
        for k in range(half):
            column = pl.multiple_of(lax.rem(s + k, count) * size, size)
            whole[pl.ds(row, size), pl.ds(column, size)] = ref[base + k * size : base + (k + 1) * size, :]
        a = lax.rem(s, half)
        row = pl.multiple_of(a * size + lax.div(s, half) * (size // 2), size // 2)
        column = pl.multiple_of((a + half) * size, size)
        start = base + half * size
        whole[pl.ds(row, size // 2), pl.ds(column, size)] = ref[start : start + size // 2, :]


def by_symmetric(a, whole):
    return nn(a, whole) + nt(a, whole)


def two_rows(row):
    high = row.astype(BF16).astype(F32)
    index = lax.broadcasted_iota(jnp.int32, (TAIL, row.shape[1]), 0)
    return jnp.where(index == 0, high, jnp.where(index == 1, row - high, 0.0)).astype(BF16)


def one_row(tile):
    return tile[0:1].astype(F32) + tile[1:2].astype(F32)


def on_device(trans, offset, spread):
    count = lax.axis_size("row")
    _, rows, size = trans.shape
    half = count // 2
    packed = half * rows + rows // 2
    product = 2 * rows * size * size
    panel = kept((rows, size), BF16)
    wide = kept((rows, size), F32)
    pair = kept((2 * rows, size), BF16)
    whole = kept((size, size), BF16)
    short = kept((rows + TAIL, size), BF16)
    long = kept((2 * rows + TAIL, size), BF16)
    line = kept((8, rows), F32)

    def gather(block, parts):
        fore, back = [block], [block]
        for _ in range(half - 1):
            fore.append(hop(fore[-1], "row", 1))
            back.append(hop(back[-1], "row", -1))
        halves = parts[0](fore[-1]), parts[1](back[-1])
        even = hop(halves[0], "row", 1)
        odd = hop(halves[1], "row", -1)
        arrays = [block] + fore[1:] + back[1:]
        offsets = [0] + [-k for k in range(1, half)] + list(range(1, half))
        return arrays, offsets, even, odd, halves

    e_arrays, offsets, e_even_last, e_odd_last, e_halves = gather(
        trans, (lambda x: part(x, 0, (rows, size)), lambda x: part(x, 1, (rows, size)))
    )
    b1_in = hop(part(trans, 1, (rows, size)), "tm", 1)

    def pack(l_ref, g_ref, out):
        z = lax.axis_index("row")
        for b in range(2):
            base = b * (packed + TAIL)
            for k in range(half):
                c = lax.rem(z + k, count)
                tile = l_ref[b, :, pl.ds(pl.multiple_of(c * rows, rows), rows)]
                out[base + k * rows : base + (k + 1) * rows, :] = tile * jnp.asarray(0.5, BF16) if k == 0 else tile
            c = lax.rem(z + half, count)
            tile = l_ref[b, :, pl.ds(pl.multiple_of(c * rows, rows), rows)].astype(F32)
            lower = tile.T[rows // 2 :]
            out[base + half * rows : base + packed, :] = jnp.where(z < half, tile[: rows // 2], lower).astype(BF16)
        g = g_ref[...].astype(F32)
        index = lax.broadcasted_iota(jnp.int32, (TAIL, rows), 0)
        tile = jnp.where(index == 0, g[0:1], jnp.where(index == 1, g[1:2], 0.0))
        out[packed : packed + TAIL, :] = tile.astype(BF16)

    (sent,) = call(pack, [spread, offset], [kept((2 * packed + TAIL, rows), BF16)], 1000)
    l_arrays, _, l_even_last, l_odd_last, _ = gather(
        sent,
        (
            lambda x: part(x, slice(0, packed + TAIL), (packed + TAIL, rows), e_halves),
            lambda x: part(x, slice(packed + TAIL, 2 * packed + TAIL), (packed, rows), e_halves),
        ),
    )
    n = len(l_arrays)

    def first(*refs):
        even_last, odd_last, b1_ref, out, b2_ref, even, odd = refs[n:]
        past = lax.axis_index("tm") < 1
        join([(way, ref[0]) for way, ref in zip(offsets, refs)] + [(half, even_last[...])], even, count)
        b1 = b1_ref[...]
        b2 = nn(b1, even[...]).astype(BF16)
        b2_ref[...] = b2
        join([(way, ref[1]) for way, ref in zip(offsets, refs)] + [(half, odd_last[...])], odd, count)
        both = nn(jnp.concatenate([refs[0][0], b2], axis=0), odd[...])
        out[:rows, :] = both[:rows].astype(BF16)
        out[rows:, :] = jnp.where(past, b1.astype(F32), both[rows:]).astype(BF16)

    m, b2, e_even, e_odd = call(
        first, e_arrays + [e_even_last, e_odd_last, b1_in], [pair, panel, whole, whole], 3 * product
    )
    m_in = hop(m, "tm", 1)

    def opened(*refs):
        last, b1_ref = refs[n : n + 2]
        close_ref, l_ev, g_ref = refs[n + 2 :]
        unpack([(way, (ref, 0)) for way, ref in zip(offsets, refs)] + [(half, (last, 0))], l_ev, count)
        for way, ref in list(zip(offsets, refs)) + [(half, last)]:
            column = pl.multiple_of(slot(way, count) * rows, rows)
            g_ref[:, pl.ds(column, rows)] = ref[packed : packed + TAIL, :]
        close_ref[...] = by_symmetric(b1_ref[...], l_ev[...])

    close, l_even, g_all = call(
        opened,
        l_arrays + [l_even_last, b1_in],
        [wide, whole, kept((TAIL, size), BF16)],
        2 * product,
        after=(m,),
    )

    def odds(*refs):
        last, b1_ref, b2_ref, own, g_ref = refs[n : n + 5]
        far_ref, head_ref, line_ref, l_od = refs[n + 5 :]
        unpack([(way, (ref, packed + TAIL)) for way, ref in zip(offsets, refs)] + [(half, (last, 0))], l_od, count)
        g = g_ref[...]
        far = by_symmetric(jnp.concatenate([own[0], b2_ref[...]], axis=0), l_od[...])
        head_ref[...] = far[:rows]
        far_ref[...] = far[rows:]
        index = lax.broadcasted_iota(jnp.int32, (8, rows), 0)
        row = nt(g, b1_ref[...])[0:1] + nt(g, b2_ref[...])[1:2]
        line_ref[...] = jnp.where(index == 0, row, nt(g, own[0])[1:2])

    far, head, line_, l_odd = call(
        odds,
        l_arrays + [l_odd_last, b1_in, b2, trans, g_all],
        [wide, wide, line, whole],
        4 * product,
        after=(close,),
    )

    def fourth(m_ref, l_ev, g_ref, out):
        past = lax.axis_index("tm") < 2
        own = m_ref[rows:, :]
        out[:rows, :] = jnp.where(past, 0.0, by_symmetric(own, l_ev[...])).astype(BF16)
        out[rows:, :] = jnp.zeros((TAIL, size), BF16)
        out[rows:, :rows] = two_rows(jnp.where(past, 0.0, nt(g_ref[...], own)[0:1]))

    (v,) = call(fourth, [m_in, l_even, g_all], [short], 2 * product, after=(line_,))
    v_in = hop(v, "tm", -1)

    def third(m_ref, even, odd, l_ev, l_od, g_ref, out):
        past = lax.axis_index("tm") < 1
        one = m_ref[:rows, :]
        two = nn(one, even[...]).astype(BF16)
        three = jnp.where(past, one.astype(F32), nn(two, odd[...]))
        far = by_symmetric(two, l_od[...])
        w = by_symmetric(one, l_ev[...]) + nt(far.astype(BF16), even[...])
        row = nt(g_ref[...], one)[0:1] + nt(g_ref[...], two)[1:2]
        out[:rows, :] = jnp.where(past, 0.0, w).astype(BF16)
        out[rows : 2 * rows, :] = three.astype(BF16)
        out[2 * rows :, :] = jnp.zeros((TAIL, size), BF16)
        out[2 * rows :, :rows] = two_rows(jnp.where(past, 0.0, row))

    (w,) = call(third, [m_in, e_even, e_odd, l_even, l_odd, g_all], [long], 7 * product, after=(v,))
    w_in = hop(w, "tm", -1)

    def fifth(m_ref, even, b4_ref):
        own = m_ref[rows:, :]
        past = lax.axis_index("tm") < 2
        b4_ref[...] = jnp.where(past, own.astype(F32), nn(own, even[...])).astype(BF16)

    (b4,) = call(fifth, [m_in, e_even], [panel], product, after=(w,))
    b4_in = hop(b4, "tm", -2)

    def sixth(v_ref, close_ref, far_ref, line_ref, even, odd, m_ref):
        past = lax.axis_index("tm") < 1
        behind = far_ref[...] + nt(v_ref[:rows, :], odd[...])
        u = close_ref[...] + nt(behind.astype(BF16), even[...])
        row = line_ref[0:1] + one_row(v_ref[rows:, :rows])
        m_ref[:rows, :] = jnp.where(past, 0.0, u).astype(BF16)
        m_ref[rows:, :] = jnp.zeros((TAIL, size), BF16)
        m_ref[rows:, :rows] = two_rows(jnp.where(past, 0.0, row))

    (u,) = call(sixth, [v_in, close, far, line_, e_even, e_odd], [short], 2 * product, after=(b4,))
    u_in = hop(u, "tm", -1)

    def seventh(w_ref, head_ref, even, odd, l_own, out):
        inner = head_ref[...] + nt(w_ref[:rows, :], odd[...])
        out[...] = (nt(inner.astype(BF16), even[...]) + l_own[0].astype(F32)).astype(BF16)

    (l_first,) = call(seventh, [w_in, head, e_even, e_odd, spread], [panel], 2 * product, after=(u,))

    def eighth(w_ref, u_ref, b4_ref, line_ref, odd, l_ref, l_own, g_own, e_out, g_out, l_out):
        l_out[1] = (nt(u_ref[:rows, :], odd[...]) + l_own[1].astype(F32)).astype(BF16)
        l_out[0] = l_ref[...]
        e_out[0] = w_ref[rows : 2 * rows, :]
        e_out[1] = b4_ref[...]
        g = g_own[...].astype(F32)
        g_out[0:1, :] = (g[0:1] + line_ref[1:2] + one_row(w_ref[2 * rows :, :rows])).astype(BF16)
        g_out[1:2, :] = (g[1:2] + one_row(u_ref[rows:, :rows])).astype(BF16)

    return call(
        eighth,
        [w_in, u_in, b4_in, line_, e_odd, l_first, spread, offset],
        [jax.ShapeDtypeStruct(x.shape, BF16) for x in (trans, offset, spread)],
        product,
    )


def solution(mesh):
    placed = (P("tm", "row", None), P("tm", "row"), P("tm", "row", None))
    return jax.shard_map(on_device, mesh=mesh, in_specs=placed, out_specs=placed, check_vma=False)
```
